256 devices in a mesh: context: 32 (over z, x_lo, core), tensor: 8 (over x_hi, y).
Axes of the slice: x: 4 (x_hi: 2, x_lo: 2; x = x_hi * 2 + x_lo), y: 4, z: 8, core: 2. Of those that a mesh axis runs over, the one named last changes fastest.
Arguments:
- activations: bfloat16 [6144, 5120], P(('context', 'tensor')), may hold values from -6 to 6
- queries: bfloat16 [6144, 5120], P('context', 'tensor'), may hold values from -44 to 44
- key_weight: bfloat16 [5120, 1024], P(None, 'tensor'), may hold values from -0.5 to 1.1
- value_projection_weight: bfloat16 [5120, 1024], P(None, 'tensor'), may hold values from -0.078125 to 0.078125
- output_gradient: bfloat16 [6144, 5120], P('context', 'tensor'), may hold values from -6 to 6
- span_order: int32 [64], replicated, may hold values from 0 to 63, as said below
- doc_ids: int32 [6144], replicated, may hold values from 0 to 4, as said below
Outputs:
- attended: bfloat16 [6144, 5120], P('context', 'tensor')
- grad_queries: bfloat16 [6144, 5120], P('context', 'tensor')
- grad_inputs: bfloat16 [6144, 5120], P(('context', 'tensor'))
- grad_key_weight: float32 [5120, 1024], P('context', 'tensor')
- grad_value_weight: float32 [5120, 1024], P('context', 'tensor')
The draws below stay inside these ranges and needn't reach their ends.
Inputs may be any that keep to these rules, and one draw needn't show every extreme that they name: `span_order`: each number once. `doc_ids`: taken in order of positions, the document numbers never fall; one document holds exactly 3072 positions and none holds more.
All inputs are finite; a program needn't handle non-finite values.
Results may differ from the reference program's by a relative error of at most 0.02.
Values may be sent and summed in bfloat16 or wider, within the bound.
No kernel may reach another device: no remote copies, remote signals or barrier semaphores. Data moves between devices by JAX's collectives and lax.ppermute only.
A program may use at most 192 MiB of HBM per device.

```python
import math
import jax
import jax.numpy as jnp
from jax import lax

MODEL_WIDTH = 5120
QUERY_HEADS = 40
KEY_VALUE_HEADS = 8
HEAD_SIZE = 128
SPAN = 96
SPANS = 64
PACK_TOKENS = 6144


def span_perm(key):
    return jax.random.permutation(jax.random.fold_in(key, 3), SPANS).astype(jnp.int32)


def draw_span_order(key, part):
    return span_perm(key)


def draw_doc_ids(key, part):
    span_list = span_perm(key)
    long_len = PACK_TOKENS // 2
    first_key, second_key, third_key = jax.random.split(jax.random.fold_in(key, 5), 3)
    long_start = jax.random.randint(first_key, (), 2, PACK_TOKENS - long_len - 1)
    first_cut = jax.random.randint(second_key, (), 1, long_start)
    second_cut = jax.random.randint(third_key, (), long_start + long_len, PACK_TOKENS - 1)
    position = jnp.arange(PACK_TOKENS, dtype=jnp.int32)
    doc_by_pos = (position >= first_cut).astype(jnp.int32) + (position >= long_start).astype(jnp.int32) + (position >= long_start + long_len).astype(jnp.int32) + (position >= second_cut).astype(jnp.int32)
    row_pos = span_list[position // SPAN] * SPAN + position % SPAN
    return doc_by_pos[row_pos].astype(jnp.int32)


def draw_pair(key):
    keys_list = jax.random.split(jax.random.fold_in(key, 9), 2)
    inputs = jnp.clip(jax.random.normal(keys_list[0], (PACK_TOKENS, MODEL_WIDTH), jnp.float32), -6.0, 6.0)
    queries = jnp.clip(jax.random.normal(keys_list[1], (PACK_TOKENS, QUERY_HEADS * HEAD_SIZE), jnp.float32), -6.0, 6.0)
    return (inputs, queries)


def draw_activations(key, part):
    return draw_pair(key)[0].astype(jnp.bfloat16)


def draw_queries(key, part):
    return draw_pair(key)[1].astype(jnp.bfloat16)


def draw_key_weight(key, part):
    spread_portion = jnp.clip(jax.random.normal(jax.random.fold_in(key, 13), (MODEL_WIDTH, KEY_VALUE_HEADS * HEAD_SIZE), jnp.float32), -4.0, 4.0) / math.sqrt(MODEL_WIDTH)
    return spread_portion.astype(jnp.bfloat16)


def steps_of(rng, extent, shards, smallest, high):
    level, own = 1.0, jax.random.fold_in(rng, 6)
    for dim, blocks in shards:
        steps = jnp.exp(jax.random.uniform(jax.random.fold_in(own, dim), (blocks,), jnp.float32, smallest / len(shards), high / len(shards)))
        level = level * jnp.repeat(steps, extent[dim] // blocks).reshape([-1 if axis == dim else 1 for axis in range(len(extent))])
    return level


def scatter_about(key, dims, width, most, cuts=(), kind=jnp.bfloat16):
    gain = steps_of(key, dims, cuts, -0.22, 0.18) if cuts else 1.0
    drawn = jax.random.normal(key, dims, jnp.float32) * width * gain
    return jnp.minimum(jnp.maximum(drawn, -most), most).astype(kind)


def setup_inputs(seed: int = 0) -> dict:
    splits = jax.random.split(jax.random.key(seed), 8)
    activations = draw_activations(jax.random.fold_in(splits[7], 71), 0)
    queries = draw_queries(jax.random.fold_in(splits[7], 71), 0)
    key_weight = draw_key_weight(jax.random.fold_in(splits[7], 71), 0)
    value_projection_weight = scatter_about(splits[3], (MODEL_WIDTH, KEY_VALUE_HEADS * HEAD_SIZE), MODEL_WIDTH ** -0.5, 0.078125, ((1, 8),))
    output_gradient = scatter_about(splits[4], (PACK_TOKENS, QUERY_HEADS * HEAD_SIZE), 1.0, 6.0, ((0, 32), (1, 8)))
    span_order = draw_span_order(jax.random.fold_in(splits[7], 71), 0)
    doc_ids = draw_doc_ids(jax.random.fold_in(splits[7], 71), 0)
    return {"activations": activations, "queries": queries, "key_weight": key_weight, "value_projection_weight": value_projection_weight, "output_gradient": output_gradient, "span_order": span_order, "doc_ids": doc_ids}


def token_positions(span_order, seq_len):
    row_ids = jnp.arange(seq_len, dtype=jnp.int32)
    return (span_order[row_ids // SPAN] * SPAN + row_ids % SPAN).astype(jnp.int32)

def rounded(values_in):
    return lax.optimization_barrier(values_in.astype(jnp.bfloat16)).astype(jnp.float32)

def head_pass(operands, positions, doc_ids):
    query_group, key_col, value_col, grad_group = operands
    inv_root = 1.0 / math.sqrt(HEAD_SIZE)
    block_rows = 4 * SPAN
    n_blocks = PACK_TOKENS // block_rows
    heads_per_group = query_group.shape[1]
    key_f = key_col.astype(jnp.float32)
    value_f = value_col.astype(jnp.float32)

    def block_step(running, inputs):
        key_gradient, value_gradient = running
        query_b, grad_b, pos_b, doc_b = inputs
        pair_mask = ((doc_b[:, None] == doc_ids[None, :]) & (positions[None, :] <= pos_b[:, None]))[:, None, :]
        query_f = query_b.astype(jnp.float32)
        grad_f = grad_b.astype(jnp.float32)
        scores = jnp.einsum('sjd,nd->sjn', query_f, key_f) * inv_root
        row_max = lax.optimization_barrier(jnp.max(jnp.where(pair_mask, scores, -1e+30), axis=2))
        expd = jnp.where(pair_mask, jnp.exp(scores - row_max[:, :, None]), 0.0)
        row_total = lax.optimization_barrier(jnp.sum(expd, axis=2))
        attended = (jnp.einsum('sjn,nd->sjd', rounded(expd), value_f) / row_total[:, :, None]).astype(jnp.bfloat16)
        log_totals = row_max + jnp.log(row_total)
        row_delta = lax.optimization_barrier(jnp.sum(grad_f * attended.astype(jnp.float32), axis=2))
        probs = jnp.where(pair_mask, jnp.exp(scores - log_totals[:, :, None]), 0.0)
        value_gradient = value_gradient + jnp.einsum('sjn,sjd->nd', rounded(probs), grad_f)
        grad_probs = jnp.einsum('sjd,nd->sjn', grad_f, value_f)
        grad_scores = rounded(probs * (grad_probs - row_delta[:, :, None]) * inv_root)
        grad_q = jnp.einsum('sjn,nd->sjd', grad_scores, key_f).astype(jnp.bfloat16)
        key_gradient = key_gradient + jnp.einsum('sjn,sjd->nd', grad_scores, query_f)
        return ((key_gradient, value_gradient), (attended, grad_q))
    inputs = (query_group.reshape(n_blocks, block_rows, heads_per_group, HEAD_SIZE), grad_group.reshape(n_blocks, block_rows, heads_per_group, HEAD_SIZE), positions.reshape(n_blocks, block_rows), doc_ids.reshape(n_blocks, block_rows))
    zero_rows = jnp.zeros((PACK_TOKENS, HEAD_SIZE), jnp.float32)
    (key_gradient, value_gradient), (attended, grad_q) = lax.scan(block_step, (zero_rows, zero_rows), inputs)
    return (key_gradient.astype(jnp.bfloat16), value_gradient.astype(jnp.bfloat16), attended.reshape(PACK_TOKENS, heads_per_group, HEAD_SIZE), grad_q.reshape(PACK_TOKENS, heads_per_group, HEAD_SIZE))

def reference(activations, queries, key_weight, value_projection_weight, output_gradient, span_order, doc_ids):
    heads_per_group = QUERY_HEADS // KEY_VALUE_HEADS
    projected_key_rows = jnp.dot(activations, key_weight, preferred_element_type=jnp.float32).astype(jnp.bfloat16)
    projected_value_rows = jnp.dot(activations, value_projection_weight, preferred_element_type=jnp.float32).astype(jnp.bfloat16)
    positions = token_positions(span_order, PACK_TOKENS)
    query_heads_split = queries.reshape(PACK_TOKENS, KEY_VALUE_HEADS, heads_per_group, HEAD_SIZE).transpose(1, 0, 2, 3)
    gradient_split = output_gradient.reshape(PACK_TOKENS, KEY_VALUE_HEADS, heads_per_group, HEAD_SIZE).transpose(1, 0, 2, 3)
    key_heads_split = projected_key_rows.reshape(PACK_TOKENS, KEY_VALUE_HEADS, HEAD_SIZE).transpose(1, 0, 2)
    value_heads_split = projected_value_rows.reshape(PACK_TOKENS, KEY_VALUE_HEADS, HEAD_SIZE).transpose(1, 0, 2)
    key_gradient, value_gradient, attended, grad_q = lax.map(lambda operands: head_pass(operands, positions, doc_ids), (query_heads_split, key_heads_split, value_heads_split, gradient_split))
    attended = attended.transpose(1, 0, 2, 3).reshape(PACK_TOKENS, QUERY_HEADS * HEAD_SIZE)
    grad_queries = grad_q.transpose(1, 0, 2, 3).reshape(PACK_TOKENS, QUERY_HEADS * HEAD_SIZE)
    gradient_of_keys = key_gradient.transpose(1, 0, 2).reshape(PACK_TOKENS, KEY_VALUE_HEADS * HEAD_SIZE)
    gradient_of_values = value_gradient.transpose(1, 0, 2).reshape(PACK_TOKENS, KEY_VALUE_HEADS * HEAD_SIZE)
    grad_inputs = (jnp.dot(gradient_of_keys, key_weight.T, preferred_element_type=jnp.float32) + jnp.dot(gradient_of_values, value_projection_weight.T, preferred_element_type=jnp.float32)).astype(jnp.bfloat16)
    grad_key_weight = jnp.dot(activations.T, gradient_of_keys, preferred_element_type=jnp.float32)
    grad_value_weight = jnp.dot(activations.T, gradient_of_values, preferred_element_type=jnp.float32)
    return (attended, grad_queries, grad_inputs, grad_key_weight, grad_value_weight)
```

```python
import functools
import math

import jax
import jax.numpy as jnp
from jax import lax
from jax.experimental import pallas as pl
from jax.experimental.pallas import tpu as pltpu
from jax.sharding import Mesh, PartitionSpec as P


HEAD = 128
SPAN = 96
GROUP = 4
BLOCK = GROUP * SPAN
CTX = ("z", "xl", "c")
TEN = ("xh", "y")
MASKED = -1e30


def brought(n_z):
    far = n_z // 2
    steps = [0] + [s * k for k in range(1, far) for s in (1, -1)]
    return [(k, side) for k in steps for side in (0, 1)] + [(far, 0), (far, 1)]


def attention_kernel(n_near, table_ref, limit_ref, q_ref, g_ref, *refs):
    blocks, refs = refs[: 2 * n_near], refs[2 * n_near :]
    att_ref, gq_ref = refs[:2]
    outs, (kv_s, acc_s, s_s, qs, gs) = refs[2:10], refs[10:]
    halves = q_ref.shape[0] // SPAN
    n_slots = outs[0].shape[0]
    n_spans = len(outs) * n_slots
    heads = q_ref.shape[1] // HEAD
    rows = heads * SPAN
    wide = qs.shape[0]
    inv_root = 1.0 / math.sqrt(HEAD)
    scale2 = inv_root * math.log2(math.e)

    def span_at(entry):
        return pl.ds(pl.multiple_of(table_ref[entry] * SPAN, SPAN), SPAN)

    entry = 0
    for ref in blocks:
        for j in range(ref.shape[0]):
            for i in range(halves):
                kv_s[span_at(entry), :] = ref[j, i * SPAN : (i + 1) * SPAN]
                entry += 1

    def clear(p, carry):
        acc_s[pl.ds(pl.multiple_of(p * SPAN, SPAN), SPAN), :] = jnp.zeros(
            (SPAN, 2 * HEAD), jnp.float32
        )
        return carry

    lax.fori_loop(0, n_spans, clear, 0)
    qs[rows:, :] = jnp.zeros((wide - rows, HEAD), qs.dtype)
    gs[rows:, :] = jnp.zeros((wide - rows, HEAD), gs.dtype)

    for i in range(q_ref.shape[0] // SPAN):
        own = slice(i * SPAN, (i + 1) * SPAN)
        for h in range(heads):
            qs[h * SPAN : (h + 1) * SPAN, :] = q_ref[own, h * HEAD : (h + 1) * HEAD]
            gs[h * SPAN : (h + 1) * SPAN, :] = g_ref[own, h * HEAD : (h + 1) * HEAD]
        lo = table_ref[2 * n_spans + 2 * i]
        hi = table_ref[2 * n_spans + 2 * i + 1] + 1
        first = limit_ref[2 * i : 2 * i + 1, :]
        last = limit_ref[2 * i + 1 : 2 * i + 2, :]

        def block(b):
            return pl.ds(pl.multiple_of(b * BLOCK, BLOCK), BLOCK)

        def score(b, top):
            s = lax.dot_general(
                kv_s[block(b), :HEAD], qs[...], (((1,), (1,)), ((), ())),
                preferred_element_type=jnp.float32,
            ) * scale2
            pos = lax.broadcasted_iota(jnp.int32, s.shape, 0) + b * BLOCK
            s = jnp.where((pos >= first) & (pos <= last), s, MASKED)
            s_s[block(b), :] = s
            return jnp.maximum(top, jnp.max(s.reshape(BLOCK // 8, 8, wide), axis=0))

        top = lax.fori_loop(lo, hi, score, jnp.full((8, wide), MASKED, jnp.float32))
        top = jnp.max(top, axis=0, keepdims=True)

        def weigh(b, carry):
            total, summed = carry
            e = jnp.exp2(s_s[block(b), :] - top)
            s_s[block(b), :] = e
            total = total + jnp.sum(e.reshape(BLOCK // 8, 8, wide), axis=0)
            summed = summed + lax.dot_general(
                kv_s[block(b), HEAD:], e.astype(jnp.bfloat16), (((0,), (0,)), ((), ())),
                preferred_element_type=jnp.float32,
            )
            return total, summed

        total, summed = lax.fori_loop(
            lo, hi, weigh,
            (jnp.zeros((8, wide), jnp.float32), jnp.zeros((HEAD, wide), jnp.float32)),
        )
        share = 1.0 / jnp.sum(total, axis=0, keepdims=True)
        att = (summed * share).astype(jnp.bfloat16).astype(jnp.float32)
        delta = jnp.sum(att * gs[...].astype(jnp.float32).T, axis=0, keepdims=True)
        att = att.T.astype(jnp.bfloat16)

        def back(b, grad_q):
            k = kv_s[block(b), :HEAD]
            v = kv_s[block(b), HEAD:]
            p = s_s[block(b), :] * share
            grad_p = lax.dot_general(
                v, gs[...], (((1,), (1,)), ((), ())), preferred_element_type=jnp.float32
            )
            grad_s = (p * (grad_p - delta) * inv_root).astype(jnp.bfloat16)
            acc_s[block(b), HEAD:] += jnp.dot(
                p.astype(jnp.bfloat16), gs[...], preferred_element_type=jnp.float32
            )
            acc_s[block(b), :HEAD] += jnp.dot(
                grad_s, qs[...], preferred_element_type=jnp.float32
            )
            return grad_q + lax.dot_general(
                k, grad_s, (((0,), (0,)), ((), ())), preferred_element_type=jnp.float32
            )

        grad_q = lax.fori_loop(lo, hi, back, jnp.zeros((HEAD, wide), jnp.float32))
        grad_q = grad_q.T.astype(jnp.bfloat16)
        for h in range(heads):
            att_ref[own, h * HEAD : (h + 1) * HEAD] = att[h * SPAN : (h + 1) * SPAN]
            gq_ref[own, h * HEAD : (h + 1) * HEAD] = grad_q[h * SPAN : (h + 1) * SPAN]

    def send(j, carry):
        for k, out in enumerate(outs):
            out[j] = acc_s[span_at(n_spans + k * n_slots + j), :].astype(jnp.bfloat16)
        return carry

    lax.fori_loop(0, n_slots, send, 0)


def attend(table, limit, queries, grads, near, far):
    smem = pl.BlockSpec(memory_space=pltpu.SMEM)
    vmem = pl.BlockSpec(memory_space=pltpu.VMEM)
    shard = queries.shape[0]
    n_slots = sum(x.shape[0] for x in near) // 2
    tokens = 4 * n_slots * shard
    wide = limit.shape[1]
    part = jax.ShapeDtypeStruct((n_slots, SPAN, 2 * HEAD), jnp.bfloat16)
    rows_like = jax.ShapeDtypeStruct(queries.shape, jnp.bfloat16)
    return pl.pallas_call(
        functools.partial(attention_kernel, len(near)),
        name="attention",
        out_shape=(rows_like, rows_like) + (part,) * 8,
        in_specs=[smem] + [vmem] * (3 + len(near) + len(far)),
        out_specs=[vmem] * 10,
        scratch_shapes=[
            pltpu.VMEM((tokens, 2 * HEAD), jnp.bfloat16),
            pltpu.VMEM((tokens, 2 * HEAD), jnp.float32),
            pltpu.VMEM((tokens, wide), jnp.float32),
            pltpu.VMEM((wide, HEAD), jnp.bfloat16),
            pltpu.VMEM((wide, HEAD), jnp.bfloat16),
        ],
    )(table, limit, queries, grads, *near, *far)


def strips_kernel(at_ref, rows_ref, keep_ref, give_c_ref, give_x_ref, turned):
    n_z, part, _ = keep_ref.shape
    for i in range(n_z):
        turned[...] = rows_ref[:, i * 4 * part : (i + 1) * 4 * part].astype(jnp.float32).T
        for ref, slot, k in (
            (keep_ref, i, 0),
            (give_c_ref, i, 1),
            (give_x_ref, i, 2),
            (give_c_ref, n_z + i, 3),
        ):
            start = pl.multiple_of(at_ref[k] * part, 16)
            ref[slot] = turned[pl.ds(start, part), :].astype(jnp.bfloat16)


def strips_of(at, rows, n_z):
    shard, width = rows.shape
    part = width // (4 * n_z)
    vmem = pl.BlockSpec(memory_space=pltpu.VMEM)

    def like(n):
        return jax.ShapeDtypeStruct((n, part, shard), jnp.bfloat16)

    return pl.pallas_call(
        strips_kernel,
        name="strips",
        out_shape=(like(n_z), like(2 * n_z), like(n_z)),
        in_specs=[pl.BlockSpec(memory_space=pltpu.SMEM), vmem],
        out_specs=[vmem] * 3,
        scratch_shapes=[pltpu.VMEM((4 * part, shard), jnp.float32)],
    )(at, rows)


def grad_w_kernel(z_ref, a_ref, b_ref, c_ref, d_ref, own_ref, far_ref, side_ref, own_out, *outs):
    n_z = a_ref.shape[0]
    for k, out in enumerate((own_out, *outs)):
        i = lax.rem(z_ref[0] + k, n_z)
        total = jnp.dot(a_ref[i], own_ref[...], preferred_element_type=jnp.float32)
        total += jnp.dot(b_ref[i], far_ref[0], preferred_element_type=jnp.float32)
        total += jnp.dot(c_ref[i], side_ref[...], preferred_element_type=jnp.float32)
        total += jnp.dot(d_ref[i], far_ref[1], preferred_element_type=jnp.float32)
        out[...] = total.astype(out.dtype)


def grad_w_parts(z, strips, own, far, side):
    n_z, part, _ = strips[0].shape
    vmem = pl.BlockSpec(memory_space=pltpu.VMEM)
    shape = (part, own.shape[1])
    return pl.pallas_call(
        grad_w_kernel,
        name="grad_w",
        out_shape=(jax.ShapeDtypeStruct(shape, jnp.float32),)
        + (jax.ShapeDtypeStruct(shape, jnp.bfloat16),) * (n_z - 1),
        in_specs=[pl.BlockSpec(memory_space=pltpu.SMEM)] + [vmem] * 7,
        out_specs=[vmem] * n_z,
    )(z, *strips, own, far, side)


def on_device(
    n_z, activations, queries, key_weight, value_weight, output_gradient, span_order, doc_ids
):
    n_ten = 8
    own_rows, width = activations.shape
    shard = own_rows * n_ten
    spans = span_order.shape[0]
    per_shard = shard // SPAN
    heads = queries.shape[1] // HEAD
    z, xl, c = (lax.axis_index(a) for a in CTX)
    swap = [(0, 1), (1, 0)]
    up = [(i, (i + 1) % n_z) for i in range(n_z)]
    down = [(i, (i - 1) % n_z) for i in range(n_z)]

    dz = jnp.array([d for d, _ in brought(n_z)], jnp.int32)
    side = jnp.array([x for _, x in brought(n_z)], jnp.int32)
    halves = jnp.arange(per_shard, dtype=jnp.int32)
    in_near = (((z - dz) % n_z) * 4 + (xl ^ side) * 2)[:, None] * per_shard + halves[None, :]
    out_z = jnp.arange(n_z, dtype=jnp.int32)
    out_side = xl ^ jnp.arange(2, dtype=jnp.int32)
    out_near = (out_z[None, None, :] * 4 + out_side[None, :, None] * 2) * per_shard
    out_near = out_near + halves[:, None, None]
    spans_of = jnp.concatenate(
        [
            (in_near + c * per_shard).reshape(-1),
            (in_near + (1 - c) * per_shard).reshape(-1),
            (out_near + c * per_shard).reshape(-1),
            (out_near + (1 - c) * per_shard).reshape(-1),
        ]
    )
    ids = jnp.arange(spans, dtype=jnp.int32)
    places = jnp.sum(jnp.where(spans_of[:, None] == ids[None, :], span_order[None, :], 0), axis=1)
    first_row = (z * 4 + xl * 2 + c) * shard
    my_order = lax.dynamic_slice_in_dim(span_order, first_row // SPAN, per_shard)
    my_doc = lax.dynamic_slice_in_dim(doc_ids, first_row, shard)
    my_first = jnp.sum((doc_ids[None, :] < my_doc[:, None]).astype(jnp.int32), axis=1)
    my_first = my_first.reshape(per_shard, SPAN)
    my_pos = my_order[:, None] * SPAN + jnp.arange(SPAN, dtype=jnp.int32)[None, :]
    bound = jnp.stack([jnp.min(my_first, axis=1) // BLOCK, my_pos[:, -1] // BLOCK], axis=1)
    table = jnp.concatenate([places, bound.reshape(-1)])
    wide = -(-heads * SPAN // 128) * 128
    pad = wide - heads * SPAN
    limit = jnp.stack(
        [
            jnp.pad(jnp.tile(my_first, (1, heads)), ((0, 0), (0, pad)), constant_values=1),
            jnp.pad(jnp.tile(my_pos, (1, heads)), ((0, 0), (0, pad))),
        ],
        axis=1,
    ).reshape(2 * per_shard, wide)

    def low(x):
        return x.astype(jnp.bfloat16)

    def add(x, y):
        return low(x.astype(jnp.float32) + y.astype(jnp.float32))

    rows = lax.all_to_all(
        jnp.broadcast_to(activations[None], (n_ten, own_rows, width)), TEN, 0, 0
    ).reshape(shard, width)
    rows, table, limit = lax.optimization_barrier((rows, table, limit))
    kv = jnp.concatenate(
        [
            low(jnp.dot(rows, w, preferred_element_type=jnp.float32))
            for w in (key_weight, value_weight)
        ],
        axis=1,
    )
    pair = jnp.stack([kv, lax.ppermute(kv, "xl", swap)])
    pair, rows = lax.optimization_barrier((pair, rows))
    near = [pair]
    a = b = pair
    for _ in range(1, n_z // 2):
        a = lax.ppermute(a, "z", up)
        b = lax.ppermute(b, "z", down)
        near += [a, b]
    near.append(lax.ppermute(a[:1], "z", up))
    near.append(lax.ppermute(b[1:], "z", down))
    far = [lax.ppermute(x, "c", swap) for x in near]

    around = jnp.stack([xl * 2 + c, xl * 2 + 1 - c, (1 - xl) * 2 + c, (1 - xl) * 2 + 1 - c])
    keep, give_c, give_x = strips_of(around, rows, n_z)
    got_c = lax.ppermute(give_c, "c", swap)
    got_x = lax.ppermute(give_x, "xl", swap)
    got_cx = lax.ppermute(got_c[n_z:], "xl", swap)
    strips = (keep, got_c[:n_z], got_x, got_cx)

    attended, grad_queries, *parts = attend(
        table, limit, queries, output_gradient, near, far
    )

    own = []
    for i in range(per_shard):
        near_0, near_1 = parts[2 * i : 2 * i + 2]
        far_0, far_1 = parts[2 * per_shard + 2 * i : 2 * per_shard + 2 * i + 2]
        far_1 = lax.ppermute(far_1, "c", swap)
        far_0 = lax.ppermute(far_0, "c", swap)
        part = lax.ppermute(add(near_1, far_1), "xl", swap)
        part = low(near_0.astype(jnp.float32) + far_0.astype(jnp.float32) + part.astype(jnp.float32))
        part = lax.all_to_all(part, "z", 0, 0)
        own.append(low(jnp.sum(part.astype(jnp.float32), axis=0)))
    grad_kv = jnp.concatenate(own, axis=0)

    beside = lax.ppermute(grad_kv, "xl", swap)
    grad_rows = lax.dot_general(
        grad_kv[:, :HEAD], key_weight, (((1,), (1,)), ((), ())), preferred_element_type=jnp.float32
    ) + lax.dot_general(
        grad_kv[:, HEAD:], value_weight, (((1,), (1,)), ((), ())),
        preferred_element_type=jnp.float32,
    )
    grad_rows, beside = lax.optimization_barrier((low(grad_rows), beside))
    terms = lax.all_to_all(grad_rows.reshape(n_ten, own_rows, width), TEN, 0, 0)

    both = jnp.stack([grad_kv, beside])
    across = lax.ppermute(both, "c", swap)
    grad_w, *sent = grad_w_parts(z[None], strips, grad_kv, across, beside)
    for k, x in enumerate(sent, 1):
        shift = [(i, (i + k) % n_z) for i in range(n_z)]
        grad_w = grad_w + lax.ppermute(x, "z", shift).astype(jnp.float32)
    grad_inputs = low(jnp.sum(terms.astype(jnp.float32), axis=0))
    return attended, grad_queries, grad_inputs, grad_w[:, :HEAD], grad_w[:, HEAD:]


def solution(mesh):
    n_z = mesh.shape["context"] // 4
    fine = Mesh(mesh.devices.reshape(n_z, 2, 2, 2, 4), CTX + TEN)

    def body(*args):
        return on_device(n_z, *args)

    return jax.shard_map(
        body,
        mesh=fine,
        in_specs=(
            P(CTX + TEN, None),
            P(CTX, TEN),
            P(None, TEN),
            P(None, TEN),
            P(CTX, TEN),
            P(),
            P(),
        ),
        out_specs=(
            P(CTX, TEN),
            P(CTX, TEN),
            P(CTX + TEN, None),
            P(CTX, TEN),
            P(CTX, TEN),
        ),
        check_vma=False,
    )
```

```python
import functools
import math

import jax
import jax.numpy as jnp
from jax import lax
from jax.experimental import pallas as pl
from jax.experimental.pallas import tpu as pltpu
from jax.sharding import Mesh, PartitionSpec as P


HEAD = 128
SPAN = 96
GROUP = 4
BLOCK = GROUP * SPAN
CTX = ("z", "xl", "c")
TEN = ("xh", "y")
MASKED = -1e30


def brought(n_z):
    far = n_z // 2
    steps = [0] + [s * k for k in range(1, far) for s in (1, -1)]
    return [(k, side) for k in steps for side in (0, 1)] + [(far, 0), (far, 1)]


def attention_kernel(n_blocks, table_ref, limit_ref, q_ref, g_ref, *refs):
    blocks, refs = refs[:n_blocks], refs[n_blocks:]
    att_ref, gq_ref = refs[:2]
    outs, (kv_s, acc_s, s_s, qs, gs, o_s) = refs[2:8], refs[8:]
    halves = q_ref.shape[0] // SPAN
    n_spans = sum(out.shape[0] for out in outs)
    heads = q_ref.shape[1] // HEAD
    rows = heads * SPAN
    wide = qs.shape[0]
    inv_root = 1.0 / math.sqrt(HEAD)
    scale2 = inv_root * math.log2(math.e)

    def span_at(entry):
        return pl.ds(pl.multiple_of(table_ref[entry] * SPAN, SPAN), SPAN)

    entry = 0
    for ref in blocks:
        for j in range(ref.shape[0]):
            for i in range(halves):
                kv_s[span_at(entry), :] = ref[j, i * SPAN : (i + 1) * SPAN]
                entry += 1

    def clear(p, carry):
        acc_s[pl.ds(pl.multiple_of(p * SPAN, SPAN), SPAN), :] = jnp.zeros(
            (SPAN, 2 * HEAD), jnp.float32
        )
        return carry

    lax.fori_loop(0, n_spans, clear, 0)
    qs[rows:, :] = jnp.zeros((wide - rows, HEAD), qs.dtype)
    gs[rows:, :] = jnp.zeros((wide - rows, HEAD), gs.dtype)

    def one_span(i, done):
        own = pl.ds(pl.multiple_of(i * SPAN, SPAN), SPAN)
        for h in range(heads):
            qs[h * SPAN : (h + 1) * SPAN, :] = q_ref[own, h * HEAD : (h + 1) * HEAD]
            gs[h * SPAN : (h + 1) * SPAN, :] = g_ref[own, h * HEAD : (h + 1) * HEAD]
        lo, full_lo, full_hi, hi = (table_ref[2 * n_spans + 4 * i + j] for j in range(4))
        first, last = limit_ref[i, 0], limit_ref[i, 1]

        def block(b):
            return pl.ds(pl.multiple_of(b * BLOCK, BLOCK), BLOCK)

        def score(masked, b, top):
            s = lax.dot_general(
                kv_s[block(b), :HEAD], qs[...], (((1,), (1,)), ((), ())),
                preferred_element_type=jnp.float32,
            ) * scale2
            if masked:
                pos = lax.broadcasted_iota(jnp.int32, s.shape, 0) + b * BLOCK
                s = jnp.where((pos >= first) & (pos <= last), s, MASKED)
            s_s[block(b), :] = s
            return jnp.maximum(top, jnp.max(s.reshape(BLOCK // 8, 8, wide), axis=0))

        masked, plain = (functools.partial(score, m) for m in (True, False))
        top = jnp.full((8, wide), MASKED, jnp.float32)
        top = lax.fori_loop(lo, full_lo, masked, top)
        top = lax.fori_loop(full_lo, full_hi, plain, top)
        top = lax.fori_loop(full_hi, hi, masked, top)
        top = jnp.max(top, axis=0, keepdims=True)
        o_s[...] = jnp.zeros_like(o_s)

        def weigh(b, total):
            e = jnp.exp2(s_s[block(b), :] - top)
            s_s[block(b), :] = e
            o_s[...] += lax.dot_general(
                kv_s[block(b), HEAD:], e.astype(jnp.bfloat16), (((0,), (0,)), ((), ())),
                preferred_element_type=jnp.float32,
            )
            return total + jnp.sum(e.reshape(BLOCK // 8, 8, wide), axis=0)

        total = lax.fori_loop(lo, hi, weigh, jnp.zeros((8, wide), jnp.float32))
        share = 1.0 / jnp.sum(total, axis=0, keepdims=True)
        att = (o_s[...] * share).astype(jnp.bfloat16).astype(jnp.float32)
        delta = jnp.sum(att * gs[...].astype(jnp.float32).T, axis=0, keepdims=True)
        att = att.T.astype(jnp.bfloat16)
        for h in range(heads):
            att_ref[own, h * HEAD : (h + 1) * HEAD] = att[h * SPAN : (h + 1) * SPAN]
        o_s[...] = jnp.zeros_like(o_s)

        def back(b, carry):
            k = kv_s[block(b), :HEAD]
            v = kv_s[block(b), HEAD:]
            p = s_s[block(b), :] * share
            grad_p = lax.dot_general(
                v, gs[...], (((1,), (1,)), ((), ())), preferred_element_type=jnp.float32
            )
            grad_s = (p * (grad_p - delta) * inv_root).astype(jnp.bfloat16)
            acc_s[block(b), HEAD:] += jnp.dot(
                p.astype(jnp.bfloat16), gs[...], preferred_element_type=jnp.float32
            )
            acc_s[block(b), :HEAD] += jnp.dot(
                grad_s, qs[...], preferred_element_type=jnp.float32
            )
            o_s[...] += lax.dot_general(
                k, grad_s, (((0,), (0,)), ((), ())), preferred_element_type=jnp.float32
            )
            return carry

        lax.fori_loop(lo, hi, back, 0)
        grad_q = o_s[...].T.astype(jnp.bfloat16)
        for h in range(heads):
            gq_ref[own, h * HEAD : (h + 1) * HEAD] = grad_q[h * SPAN : (h + 1) * SPAN]
        return done

    lax.fori_loop(0, halves, one_span, 0)

    entry = n_spans
    for out in outs:

        def send(j, carry, out=out, entry=entry):
            out[j] = acc_s[span_at(entry + j), :].astype(jnp.bfloat16)
            return carry

        lax.fori_loop(0, out.shape[0], send, 0)
        entry += out.shape[0]


def on_chip(arrays):
    return [pltpu.with_memory_space_constraint(x, pltpu.VMEM) for x in arrays]


def attend(table, limit, queries, grads, blocks):
    smem = pl.BlockSpec(memory_space=pltpu.SMEM)
    vmem = pl.BlockSpec(memory_space=pltpu.VMEM)
    shard = queries.shape[0]
    n_slots = sum(x.shape[0] for x in blocks) // 4
    tokens = 4 * n_slots * shard
    wide = limit.shape[-1]

    def part(n):
        return pltpu.VMEM((n * n_slots, SPAN, 2 * HEAD), jnp.bfloat16)

    rows_like = jax.ShapeDtypeStruct(queries.shape, jnp.bfloat16)
    return pl.pallas_call(
        functools.partial(attention_kernel, len(blocks)),
        name="attention",
        out_shape=(rows_like, rows_like, part(1), part(1), part(1), part(1), part(2), part(2)),
        in_specs=[smem] + [vmem] * (3 + len(blocks)),
        out_specs=[vmem] * 8,
        compiler_params=pltpu.CompilerParams(vmem_limit_bytes=28 * 2**20),
        scratch_shapes=[
            pltpu.VMEM((tokens, 2 * HEAD), jnp.bfloat16),
            pltpu.VMEM((tokens, 2 * HEAD), jnp.float32),
            pltpu.VMEM((tokens, wide), jnp.float32),
            pltpu.VMEM((wide, HEAD), jnp.bfloat16),
            pltpu.VMEM((wide, HEAD), jnp.bfloat16),
            pltpu.VMEM((HEAD, wide), jnp.float32),
        ],
    )(table, limit, queries, grads, *on_chip(blocks))


def strips_kernel(at_ref, rows_ref, *refs):
    outs, turned = refs[:4], refs[4]
    n_z, part, _ = outs[0].shape
    for i in range(n_z):
        turned[...] = rows_ref[:, i * 4 * part : (i + 1) * 4 * part].astype(jnp.float32).T
        for k, out in enumerate(outs):
            start = pl.multiple_of(at_ref[k] * part, 16)
            out[i] = turned[pl.ds(start, part), :].astype(jnp.bfloat16)


def strips_of(at, rows, n_z):
    shard, width = rows.shape
    part = width // (4 * n_z)
    vmem = pl.BlockSpec(memory_space=pltpu.VMEM)
    return pl.pallas_call(
        strips_kernel,
        name="strips",
        out_shape=(jax.ShapeDtypeStruct((n_z, part, shard), jnp.bfloat16),) * 4,
        in_specs=[pl.BlockSpec(memory_space=pltpu.SMEM), vmem],
        out_specs=[vmem] * 4,
        scratch_shapes=[pltpu.VMEM((4 * part, shard), jnp.float32)],
        compiler_params=pltpu.CompilerParams(vmem_limit_bytes=10 * 2**20),
    )(at, rows)


def grad_w_kernel(z_ref, *refs):
    strips, grads, outs = refs[:4], refs[4:8], refs[8:]
    n_z = strips[0].shape[0]
    for k, out in enumerate(outs):
        i = lax.rem(z_ref[0] + k, n_z)
        total = jnp.dot(strips[0][i], grads[0][...], preferred_element_type=jnp.float32)
        for x, y in zip(strips[1:], grads[1:]):
            total += jnp.dot(x[i], y[...], preferred_element_type=jnp.float32)
        out[...] = total.astype(out.dtype)


def grad_w_parts(z, strips, grads):
    n_z, part, _ = strips[0].shape
    vmem = pl.BlockSpec(memory_space=pltpu.VMEM)
    shape = (part, grads[0].shape[1])
    return pl.pallas_call(
        grad_w_kernel,
        name="grad_w",
        out_shape=(jax.ShapeDtypeStruct(shape, jnp.float32),)
        + (jax.ShapeDtypeStruct(shape, jnp.bfloat16),) * (n_z - 1),
        in_specs=[pl.BlockSpec(memory_space=pltpu.SMEM)] + [vmem] * 8,
        out_specs=[vmem] * n_z,
        compiler_params=pltpu.CompilerParams(vmem_limit_bytes=10 * 2**20),
    )(z, *strips, *grads)


def grad_rows_kernel(grad_ref, w_ref, out_ref):
    step = w_ref.shape[0] // 8
    for i in range(8):
        at = slice(i * step, (i + 1) * step)
        out_ref[:, at] = lax.dot_general(
            grad_ref[...], w_ref[at, :], (((1,), (1,)), ((), ())),
            preferred_element_type=jnp.float32,
        ).astype(out_ref.dtype)


def grad_rows_of(grad_kv, weights):
    vmem = pl.BlockSpec(memory_space=pltpu.VMEM)
    return pl.pallas_call(
        grad_rows_kernel,
        name="grad_rows",
        out_shape=pltpu.VMEM((grad_kv.shape[0], weights.shape[0]), jnp.bfloat16),
        in_specs=[vmem, vmem],
        out_specs=vmem,
        compiler_params=pltpu.CompilerParams(vmem_limit_bytes=8 * 2**20),
    )(*on_chip((grad_kv, weights)))


def total_kernel(terms_ref, out_ref):
    total = terms_ref[0].astype(jnp.float32)
    for i in range(1, terms_ref.shape[0]):
        total += terms_ref[i].astype(jnp.float32)
    out_ref[...] = total.astype(out_ref.dtype)


def total_of(terms):
    vmem = pl.BlockSpec(memory_space=pltpu.VMEM)
    return pl.pallas_call(
        total_kernel,
        name="total",
        out_shape=jax.ShapeDtypeStruct(terms.shape[1:], terms.dtype),
        in_specs=[vmem],
        out_specs=vmem,
        compiler_params=pltpu.CompilerParams(vmem_limit_bytes=4 * 2**20),
    )(*on_chip((terms,)))


def on_device(
    n_z, activations, queries, key_weight, value_weight, output_gradient, span_order, doc_ids
):
    n_ten = 8
    own_rows, width = activations.shape
    shard = own_rows * n_ten
    spans = span_order.shape[0]
    per_shard = shard // SPAN
    heads = queries.shape[1] // HEAD
    z, xl, c = (lax.axis_index(a) for a in CTX)
    swap = [(0, 1), (1, 0)]
    up = [(i, (i + 1) % n_z) for i in range(n_z)]
    down = [(i, (i - 1) % n_z) for i in range(n_z)]

    dz = jnp.array([d for d, _ in brought(n_z)], jnp.int32)
    side = jnp.array([x for _, x in brought(n_z)], jnp.int32)
    halves = jnp.arange(per_shard, dtype=jnp.int32)
    in_near = (((z - dz) % n_z) * 4 + (xl ^ side) * 2)[:, None] * per_shard + halves[None, :]
    steps = jnp.arange(n_z, dtype=jnp.int32)
    sides = (xl ^ jnp.arange(2, dtype=jnp.int32)) * 2
    out_0 = (((z - steps) % n_z) * 4)[None, :] + sides[:, None]
    out_1 = (steps * 4)[:, None] + sides[None, :]
    spans_of = jnp.concatenate(
        [
            (in_near + c * per_shard).reshape(-1),
            (in_near + (1 - c) * per_shard).reshape(-1),
            ((out_0 + c) * per_shard).reshape(-1),
            ((out_0 + 1 - c) * per_shard).reshape(-1),
            ((out_1 + c) * per_shard + 1).reshape(-1),
            ((out_1 + 1 - c) * per_shard + 1).reshape(-1),
        ]
    )
    ids = jnp.arange(spans, dtype=jnp.int32)
    places = jnp.sum(jnp.where(spans_of[:, None] == ids[None, :], span_order[None, :], 0), axis=1)
    first_row = (z * 4 + xl * 2 + c) * shard
    my_order = lax.dynamic_slice_in_dim(span_order, first_row // SPAN, per_shard)
    my_doc = lax.dynamic_slice_in_dim(doc_ids, first_row, shard)
    my_first = jnp.sum((doc_ids[None, :] < my_doc[:, None]).astype(jnp.int32), axis=1)
    my_first = my_first.reshape(per_shard, SPAN)
    my_pos = my_order[:, None] * SPAN + jnp.arange(SPAN, dtype=jnp.int32)[None, :]
    lo, hi = jnp.min(my_first, axis=1) // BLOCK, my_pos[:, -1] // BLOCK + 1
    full_lo = jnp.minimum((jnp.max(my_first, axis=1) + BLOCK - 1) // BLOCK, hi)
    full_hi = jnp.maximum((my_pos[:, 0] + 1) // BLOCK, full_lo)
    bound = jnp.stack([lo, full_lo, full_hi, hi], axis=1)
    table = jnp.concatenate([places, bound.reshape(-1)])
    wide = -(-heads * SPAN // 128) * 128
    pad = wide - heads * SPAN
    limit = jnp.stack(
        [
            jnp.pad(jnp.tile(my_first, (1, heads)), ((0, 0), (0, pad)), constant_values=1),
            jnp.pad(jnp.tile(my_pos, (1, heads)), ((0, 0), (0, pad))),
        ],
        axis=1,
    ).reshape(per_shard, 2, 1, wide)

    def low(x):
        return x.astype(jnp.bfloat16)

    def add(x, y):
        return low(x.astype(jnp.float32) + y.astype(jnp.float32))

    rows = lax.all_to_all(
        jnp.broadcast_to(activations[None], (n_ten, own_rows, width)), TEN, 0, 0
    ).reshape(shard, width)
    weights = jnp.concatenate([key_weight, value_weight], axis=1)
    rows, weights, table, limit = lax.optimization_barrier((rows, weights, table, limit))
    kv = low(jnp.dot(rows, weights, preferred_element_type=jnp.float32))
    beside = lax.ppermute(kv, "xl", swap)
    pair = jnp.stack([kv, beside])
    near = [pair]
    a = b = pair
    for _ in range(1, n_z // 2):
        a = lax.ppermute(a, "z", up)
        b = lax.ppermute(b, "z", down)
        near += [a, b]
    a = lax.ppermute(a[:1], "z", up)
    b = lax.ppermute(b[1:], "z", down)
    near = [jnp.concatenate(near[:5]), jnp.concatenate(near[5:]), jnp.concatenate([a, b])]
    far = []
    for x in near:
        far.append(lax.ppermute(x, "c", swap))

    around = jnp.stack([xl * 2 + c, xl * 2 + 1 - c, (1 - xl) * 2 + c, (1 - xl) * 2 + 1 - c])
    keep, give_c, give_x, give_cx = strips_of(around, rows, n_z)
    got_x = lax.ppermute(give_x, "xl", swap)
    got_c, got_cx = (lax.ppermute(t, "c", swap) for t in (give_c, give_cx))
    got_cx = lax.ppermute(got_cx, "xl", swap)
    strips = (keep, got_c, got_x, got_cx)

    attended, grad_queries, *parts = attend(table, limit, queries, output_gradient, [*near, *far])

    near_00, near_01, far_00, far_01, near_1, far_1 = parts
    far_01 = lax.ppermute(far_01, "c", swap)
    far_1 = lax.ppermute(far_1, "c", swap)
    far_00 = lax.ppermute(far_00, "c", swap)
    part_0 = lax.ppermute(add(near_01, far_01), "xl", swap)
    part_1 = add(near_1, far_1).reshape(n_z, 2, SPAN, 2 * HEAD)
    part_1 = lax.all_to_all(part_1, "z", 0, 0)
    part_0 = near_00.astype(jnp.float32) + far_00.astype(jnp.float32) + part_0.astype(jnp.float32)
    own_0 = part_0[0]
    for k in sorted(range(1, n_z), key=lambda k: -min(k, n_z - k)):
        shift = [(i, (i - k) % n_z) for i in range(n_z)]
        own_0 = own_0 + lax.ppermute(low(part_0[k]), "z", shift).astype(jnp.float32)
    part_1 = jnp.sum(part_1.astype(jnp.float32), axis=0)
    own_1 = part_1[0] + lax.ppermute(low(part_1[1]), "xl", swap).astype(jnp.float32)
    grad_kv = low(jnp.concatenate([own_0, own_1], axis=0))

    beside = lax.ppermute(grad_kv, "xl", swap)
    across = lax.ppermute(grad_kv, "c", swap)
    corner = lax.ppermute(beside, "c", swap)
    grad_rows = grad_rows_of(grad_kv, weights)
    terms = lax.all_to_all(grad_rows.reshape(n_ten, own_rows, width), TEN, 0, 0)

    grad_w, *sent = grad_w_parts(z[None], strips, (grad_kv, across, beside, corner))
    sent = sorted(enumerate(sent, 1), key=lambda kx: -min(kx[0], n_z - kx[0]))
    for k, x in sent:
        shift = [(i, (i + k) % n_z) for i in range(n_z)]
        grad_w = grad_w + lax.ppermute(x, "z", shift).astype(jnp.float32)
    grad_inputs = total_of(terms)
    return attended, grad_queries, grad_inputs, grad_w[:, :HEAD], grad_w[:, HEAD:]


def solution(mesh):
    n_z = mesh.shape["context"] // 4
    fine = Mesh(mesh.devices.reshape(n_z, 2, 2, 2, 4), CTX + TEN)

    def body(*args):
        return on_device(n_z, *args)

    return jax.shard_map(
        body,
        mesh=fine,
        in_specs=(
            P(CTX + TEN, None),
            P(CTX, TEN),
            P(None, TEN),
            P(None, TEN),
            P(CTX, TEN),
            P(),
            P(),
        ),
        out_specs=(
            P(CTX, TEN),
            P(CTX, TEN),
            P(CTX + TEN, None),
            P(CTX, TEN),
            P(CTX, TEN),
        ),
        check_vma=False,
    )
```

```python
import functools
import math

import jax
import jax.numpy as jnp
from jax import lax
from jax.experimental import pallas as pl
from jax.experimental.pallas import tpu as pltpu
from jax.sharding import Mesh, PartitionSpec as P


HEAD = 128
SPAN = 96
GROUP = 4
BLOCK = GROUP * SPAN
CTX = ("z", "xl", "c")
TEN = ("xh", "y")
MASKED = -1e30


def brought(n_z):
    far = n_z // 2
    steps = [0] + [s * k for k in range(1, far) for s in (1, -1)]
    return [(k, side) for k in steps for side in (0, 1)] + [(far, 0), (far, 1)]


def attention_kernel(n_blocks, table_ref, limit_ref, q_ref, g_ref, *refs):
    blocks, refs = refs[:n_blocks], refs[n_blocks:]
    att_ref, gq_ref = refs[:2]
    outs, (kv_s, acc_s, s_s, qs, gs, o_s) = refs[2:8], refs[8:]
    halves = q_ref.shape[0] // SPAN
    n_spans = sum(out.shape[0] for out in outs)
    heads = q_ref.shape[1] // HEAD
    rows = heads * SPAN
    wide = qs.shape[0]
    inv_root = 1.0 / math.sqrt(HEAD)
    scale2 = inv_root * math.log2(math.e)

    def span_at(entry):
        return pl.ds(pl.multiple_of(table_ref[entry] * SPAN, SPAN), SPAN)

    entry = 0
    for ref in blocks:
        for j in range(ref.shape[0]):
            for i in range(halves):
                kv_s[span_at(entry), :] = ref[j, i * SPAN : (i + 1) * SPAN]
                entry += 1

    def clear(p, carry):
        acc_s[pl.ds(pl.multiple_of(p * SPAN, SPAN), SPAN), :] = jnp.zeros(
            (SPAN, 2 * HEAD), jnp.float32
        )
        return carry

    lax.fori_loop(0, n_spans, clear, 0)
    qs[rows:, :] = jnp.zeros((wide - rows, HEAD), qs.dtype)
    gs[rows:, :] = jnp.zeros((wide - rows, HEAD), gs.dtype)

    def one_span(i, done):
        own = pl.ds(pl.multiple_of(i * SPAN, SPAN), SPAN)
        for h in range(heads):
            qs[h * SPAN : (h + 1) * SPAN, :] = q_ref[own, h * HEAD : (h + 1) * HEAD]
            gs[h * SPAN : (h + 1) * SPAN, :] = g_ref[own, h * HEAD : (h + 1) * HEAD]
        lo, full_lo, full_hi, hi = (table_ref[2 * n_spans + 4 * i + j] for j in range(4))
        first, last = limit_ref[i, 0], limit_ref[i, 1]

        def block(b):
            return pl.ds(pl.multiple_of(b * BLOCK, BLOCK), BLOCK)

        def score(masked, b, top):
            s = lax.dot_general(
                kv_s[block(b), :HEAD], qs[...], (((1,), (1,)), ((), ())),
                preferred_element_type=jnp.float32,
            ) * scale2
            if masked:
                pos = lax.broadcasted_iota(jnp.int32, s.shape, 0) + b * BLOCK
                s = jnp.where((pos >= first) & (pos <= last), s, MASKED)
            s_s[block(b), :] = s
            return jnp.maximum(top, jnp.max(s.reshape(BLOCK // 8, 8, wide), axis=0))

        masked, plain = (functools.partial(score, m) for m in (True, False))
        top = jnp.full((8, wide), MASKED, jnp.float32)
        top = lax.fori_loop(lo, full_lo, masked, top)
        top = lax.fori_loop(full_lo, full_hi, plain, top)
        top = lax.fori_loop(full_hi, hi, masked, top)
        top = jnp.max(top, axis=0, keepdims=True)
        o_s[...] = jnp.zeros_like(o_s)

        def weigh(b, total):
            e = jnp.exp2(s_s[block(b), :] - top)
            s_s[block(b), :] = e
            o_s[...] += lax.dot_general(
                kv_s[block(b), HEAD:], e.astype(jnp.bfloat16), (((0,), (0,)), ((), ())),
                preferred_element_type=jnp.float32,
            )
            return total + jnp.sum(e.reshape(BLOCK // 8, 8, wide), axis=0)

        total = lax.fori_loop(lo, hi, weigh, jnp.zeros((8, wide), jnp.float32))
        share = 1.0 / jnp.sum(total, axis=0, keepdims=True)
        att = (o_s[...] * share).astype(jnp.bfloat16).astype(jnp.float32)
        delta = jnp.sum(att * gs[...].astype(jnp.float32).T, axis=0, keepdims=True)
        att = att.T.astype(jnp.bfloat16)
        for h in range(heads):
            att_ref[own, h * HEAD : (h + 1) * HEAD] = att[h * SPAN : (h + 1) * SPAN]
        o_s[...] = jnp.zeros_like(o_s)

        def back(b, carry):
            k = kv_s[block(b), :HEAD]
            v = kv_s[block(b), HEAD:]
            p = s_s[block(b), :] * share
            grad_p = lax.dot_general(
                v, gs[...], (((1,), (1,)), ((), ())), preferred_element_type=jnp.float32
            )
            grad_s = (p * (grad_p - delta) * inv_root).astype(jnp.bfloat16)
            acc_s[block(b), HEAD:] += jnp.dot(
                p.astype(jnp.bfloat16), gs[...], preferred_element_type=jnp.float32
            )
            acc_s[block(b), :HEAD] += jnp.dot(
                grad_s, qs[...], preferred_element_type=jnp.float32
            )
            o_s[...] += lax.dot_general(
                k, grad_s, (((0,), (0,)), ((), ())), preferred_element_type=jnp.float32
            )
            return carry

        lax.fori_loop(lo, hi, back, 0)
        grad_q = o_s[...].T.astype(jnp.bfloat16)
        for h in range(heads):
            gq_ref[own, h * HEAD : (h + 1) * HEAD] = grad_q[h * SPAN : (h + 1) * SPAN]
        return done

    lax.fori_loop(0, halves, one_span, 0)

    entry = n_spans
    for out in outs:

        def send(j, carry, out=out, entry=entry):
            out[j] = acc_s[span_at(entry + j), :].astype(jnp.bfloat16)
            return carry

        lax.fori_loop(0, out.shape[0], send, 0)
        entry += out.shape[0]


def on_chip(arrays):
    return [pltpu.with_memory_space_constraint(x, pltpu.VMEM) for x in arrays]


def attend(table, limit, queries, grads, blocks):
    smem = pl.BlockSpec(memory_space=pltpu.SMEM)
    vmem = pl.BlockSpec(memory_space=pltpu.VMEM)
    shard = queries.shape[0]
    n_slots = sum(x.shape[0] for x in blocks) // 4
    tokens = 4 * n_slots * shard
    wide = limit.shape[-1]

    def part(n):
        return pltpu.VMEM((n * n_slots, SPAN, 2 * HEAD), jnp.bfloat16)

    rows_like = jax.ShapeDtypeStruct(queries.shape, jnp.bfloat16)
    return pl.pallas_call(
        functools.partial(attention_kernel, len(blocks)),
        name="attention",
        out_shape=(rows_like, rows_like) + (part(2), part(1), part(1)) * 2,
        in_specs=[smem] + [vmem] * (3 + len(blocks)),
        out_specs=[vmem] * 8,
        compiler_params=pltpu.CompilerParams(vmem_limit_bytes=28 * 2**20),
        scratch_shapes=[
            pltpu.VMEM((tokens, 2 * HEAD), jnp.bfloat16),
            pltpu.VMEM((tokens, 2 * HEAD), jnp.float32),
            pltpu.VMEM((tokens, wide), jnp.float32),
            pltpu.VMEM((wide, HEAD), jnp.bfloat16),
            pltpu.VMEM((wide, HEAD), jnp.bfloat16),
            pltpu.VMEM((HEAD, wide), jnp.float32),
        ],
    )(table, limit, queries, grads, *on_chip(blocks))


def strips_kernel(at_ref, rows_ref, *refs):
    outs, turned = refs[:4], refs[4]
    n_z, part, _ = outs[0].shape
    for i in range(n_z):
        turned[...] = rows_ref[:, i * 4 * part : (i + 1) * 4 * part].astype(jnp.float32).T
        for k, out in enumerate(outs):
            start = pl.multiple_of(at_ref[k] * part, 16)
            out[i] = turned[pl.ds(start, part), :].astype(jnp.bfloat16)


def strips_of(at, rows, n_z):
    shard, width = rows.shape
    part = width // (4 * n_z)
    vmem = pl.BlockSpec(memory_space=pltpu.VMEM)
    return pl.pallas_call(
        strips_kernel,
        name="strips",
        out_shape=(jax.ShapeDtypeStruct((n_z, part, shard), jnp.bfloat16),) * 4,
        in_specs=[pl.BlockSpec(memory_space=pltpu.SMEM), vmem],
        out_specs=[vmem] * 4,
        scratch_shapes=[pltpu.VMEM((4 * part, shard), jnp.float32)],
        compiler_params=pltpu.CompilerParams(vmem_limit_bytes=10 * 2**20),
    )(at, rows)


def grad_w_kernel(z_ref, *refs):
    strips, grads, outs = refs[:4], refs[4:8], refs[8:]
    n_z = strips[0].shape[0]
    for k, out in enumerate(outs):
        i = lax.rem(z_ref[0] + k, n_z)
        total = jnp.dot(strips[0][i], grads[0][...], preferred_element_type=jnp.float32)
        for x, y in zip(strips[1:], grads[1:]):
            total += jnp.dot(x[i], y[...], preferred_element_type=jnp.float32)
        out[...] = total.astype(out.dtype)


def grad_w_parts(z, strips, grads):
    n_z, part, _ = strips[0].shape
    vmem = pl.BlockSpec(memory_space=pltpu.VMEM)
    shape = (part, grads[0].shape[1])
    return pl.pallas_call(
        grad_w_kernel,
        name="grad_w",
        out_shape=(jax.ShapeDtypeStruct(shape, jnp.float32),)
        + (jax.ShapeDtypeStruct(shape, jnp.bfloat16),) * (n_z - 1),
        in_specs=[pl.BlockSpec(memory_space=pltpu.SMEM)] + [vmem] * 8,
        out_specs=[vmem] * n_z,
        compiler_params=pltpu.CompilerParams(vmem_limit_bytes=10 * 2**20),
    )(z, *strips, *grads)


def grad_rows_kernel(grad_ref, w_ref, out_ref):
    step = w_ref.shape[0] // 8
    for i in range(8):
        at = slice(i * step, (i + 1) * step)
        out_ref[:, at] = lax.dot_general(
            grad_ref[...], w_ref[at, :], (((1,), (1,)), ((), ())),
            preferred_element_type=jnp.float32,
        ).astype(out_ref.dtype)


def grad_rows_of(grad_kv, weights):
    vmem = pl.BlockSpec(memory_space=pltpu.VMEM)
    return pl.pallas_call(
        grad_rows_kernel,
        name="grad_rows",
        out_shape=pltpu.VMEM((grad_kv.shape[0], weights.shape[0]), jnp.bfloat16),
        in_specs=[vmem, vmem],
        out_specs=vmem,
        compiler_params=pltpu.CompilerParams(vmem_limit_bytes=8 * 2**20),
    )(*on_chip((grad_kv, weights)))


def total_kernel(terms_ref, out_ref):
    total = terms_ref[0].astype(jnp.float32)
    for i in range(1, terms_ref.shape[0]):
        total += terms_ref[i].astype(jnp.float32)
    out_ref[...] = total.astype(out_ref.dtype)


def total_of(terms):
    vmem = pl.BlockSpec(memory_space=pltpu.VMEM)
    return pl.pallas_call(
        total_kernel,
        name="total",
        out_shape=jax.ShapeDtypeStruct(terms.shape[1:], terms.dtype),
        in_specs=[vmem],
        out_specs=vmem,
        compiler_params=pltpu.CompilerParams(vmem_limit_bytes=4 * 2**20),
    )(*on_chip((terms,)))


def on_device(
    n_z, activations, queries, key_weight, value_weight, output_gradient, span_order, doc_ids
):
    n_ten = 8
    own_rows, width = activations.shape
    shard = own_rows * n_ten
    spans = span_order.shape[0]
    per_shard = shard // SPAN
    heads = queries.shape[1] // HEAD
    z, xl, c = (lax.axis_index(a) for a in CTX)
    swap = [(0, 1), (1, 0)]
    up = [(i, (i + 1) % n_z) for i in range(n_z)]
    down = [(i, (i - 1) % n_z) for i in range(n_z)]

    dz = jnp.array([d for d, _ in brought(n_z)], jnp.int32)
    side = jnp.array([x for _, x in brought(n_z)], jnp.int32)
    halves = jnp.arange(per_shard, dtype=jnp.int32)
    in_near = (((z - dz) % n_z) * 4 + (xl ^ side) * 2)[:, None] * per_shard + halves[None, :]
    steps = jnp.arange(n_z, dtype=jnp.int32)
    below = ((z - steps) % n_z) * 4

    def sent_at(core):
        own_side = ((below + xl * 2 + core)[:, None] * per_shard + halves[None, :]).reshape(-1)
        first = (below + (1 - xl) * 2 + core) * per_shard
        second = (steps * 4 + (1 - xl) * 2 + core) * per_shard + 1
        return [own_side, first, second]

    spans_of = jnp.concatenate(
        [
            (in_near + c * per_shard).reshape(-1),
            (in_near + (1 - c) * per_shard).reshape(-1),
            *sent_at(c),
            *sent_at(1 - c),
        ]
    )
    ids = jnp.arange(spans, dtype=jnp.int32)
    places = jnp.sum(jnp.where(spans_of[:, None] == ids[None, :], span_order[None, :], 0), axis=1)
    first_row = (z * 4 + xl * 2 + c) * shard
    my_order = lax.dynamic_slice_in_dim(span_order, first_row // SPAN, per_shard)
    my_doc = lax.dynamic_slice_in_dim(doc_ids, first_row, shard)
    my_first = jnp.sum((doc_ids[None, :] < my_doc[:, None]).astype(jnp.int32), axis=1)
    my_first = my_first.reshape(per_shard, SPAN)
    my_pos = my_order[:, None] * SPAN + jnp.arange(SPAN, dtype=jnp.int32)[None, :]
    lo, hi = jnp.min(my_first, axis=1) // BLOCK, my_pos[:, -1] // BLOCK + 1
    full_lo = jnp.minimum((jnp.max(my_first, axis=1) + BLOCK - 1) // BLOCK, hi)
    full_hi = jnp.maximum((my_pos[:, 0] + 1) // BLOCK, full_lo)
    bound = jnp.stack([lo, full_lo, full_hi, hi], axis=1)
    table = jnp.concatenate([places, bound.reshape(-1)])
    wide = -(-heads * SPAN // 128) * 128
    pad = wide - heads * SPAN
    limit = jnp.stack(
        [
            jnp.pad(jnp.tile(my_first, (1, heads)), ((0, 0), (0, pad)), constant_values=1),
            jnp.pad(jnp.tile(my_pos, (1, heads)), ((0, 0), (0, pad))),
        ],
        axis=1,
    ).reshape(per_shard, 2, 1, wide)

    def low(x):
        return x.astype(jnp.bfloat16)

    def add(x, y):
        return low(x.astype(jnp.float32) + y.astype(jnp.float32))

    rows = lax.all_to_all(
        jnp.broadcast_to(activations[None], (n_ten, own_rows, width)), TEN, 0, 0
    ).reshape(shard, width)
    weights = jnp.concatenate([key_weight, value_weight], axis=1)
    rows, weights, table, limit = lax.optimization_barrier((rows, weights, table, limit))
    kv = low(jnp.dot(rows, weights, preferred_element_type=jnp.float32))
    beside = lax.ppermute(kv, "xl", swap)
    pair = jnp.stack([kv, beside])
    near = [pair]
    a = b = pair
    for _ in range(1, n_z // 2):
        a = lax.ppermute(a, "z", up)
        b = lax.ppermute(b, "z", down)
        near += [a, b]
    a = lax.ppermute(a[:1], "z", up)
    b = lax.ppermute(b[1:], "z", down)
    near = [jnp.concatenate(near[:5]), jnp.concatenate(near[5:]), jnp.concatenate([a, b])]
    far = []
    for x in near:
        far.append(lax.ppermute(x, "c", swap))

    around = jnp.stack([xl * 2 + c, xl * 2 + 1 - c, (1 - xl) * 2 + c, (1 - xl) * 2 + 1 - c])
    keep, give_c, give_x, give_cx = strips_of(around, rows, n_z)
    got_x = lax.ppermute(give_x, "xl", swap)
    got_c, got_cx = (lax.ppermute(t, "c", swap) for t in (give_c, give_cx))
    got_cx = lax.ppermute(got_cx, "xl", swap)
    strips = (keep, got_c, got_x, got_cx)

    attended, grad_queries, *parts = attend(table, limit, queries, output_gradient, [*near, *far])

    near_own, near_0, near_1, far_own, far_0, far_1 = parts
    far_0 = lax.ppermute(far_0, "c", swap)
    far_1 = lax.ppermute(far_1, "c", swap)
    far_own = lax.ppermute(far_own, "c", swap)
    part_0 = lax.ppermute(add(near_0, far_0), "xl", swap)
    part_1 = lax.all_to_all(add(near_1, far_1), "z", 0, 0)
    part = near_own.astype(jnp.float32) + far_own.astype(jnp.float32)
    part = part.reshape(n_z, per_shard, SPAN, 2 * HEAD)
    part += jnp.pad(part_0[:, None].astype(jnp.float32), ((0, 0), (0, 1), (0, 0), (0, 0)))
    own = part[0]
    for k in sorted(range(1, n_z), key=lambda k: -min(k, n_z - k)):
        shift = [(i, (i - k) % n_z) for i in range(n_z)]
        own = own + lax.ppermute(low(part[k]), "z", shift).astype(jnp.float32)
    part_1 = low(jnp.sum(part_1.astype(jnp.float32), axis=0))
    part_1 = lax.ppermute(part_1, "xl", swap)
    own = own + jnp.pad(part_1[None].astype(jnp.float32), ((1, 0), (0, 0), (0, 0)))
    grad_kv = low(own).reshape(shard, 2 * HEAD)

    beside = lax.ppermute(grad_kv, "xl", swap)
    across = lax.ppermute(grad_kv, "c", swap)
    corner = lax.ppermute(beside, "c", swap)
    grad_rows = grad_rows_of(grad_kv, weights)
    terms = lax.all_to_all(grad_rows.reshape(n_ten, own_rows, width), TEN, 0, 0)

    grad_w, *sent = grad_w_parts(z[None], strips, (grad_kv, across, beside, corner))
    sent = sorted(enumerate(sent, 1), key=lambda kx: -min(kx[0], n_z - kx[0]))
    for k, x in sent:
        shift = [(i, (i + k) % n_z) for i in range(n_z)]
        grad_w = grad_w + lax.ppermute(x, "z", shift).astype(jnp.float32)
    grad_inputs = total_of(terms)
    return attended, grad_queries, grad_inputs, grad_w[:, :HEAD], grad_w[:, HEAD:]


def solution(mesh):
    n_z = mesh.shape["context"] // 4
    fine = Mesh(mesh.devices.reshape(n_z, 2, 2, 2, 4), CTX + TEN)

    def body(*args):
        return on_device(n_z, *args)

    return jax.shard_map(
        body,
        mesh=fine,
        in_specs=(
            P(CTX + TEN, None),
            P(CTX, TEN),
            P(None, TEN),
            P(None, TEN),
            P(CTX, TEN),
            P(),
            P(),
        ),
        out_specs=(
            P(CTX, TEN),
            P(CTX, TEN),
            P(CTX + TEN, None),
            P(CTX, TEN),
            P(CTX, TEN),
        ),
        check_vma=False,
    )
```

```python
import functools
import math

import jax
import jax.numpy as jnp
from jax import lax
from jax.experimental import pallas as pl
from jax.experimental.pallas import tpu as pltpu
from jax.sharding import Mesh, PartitionSpec as P


HEAD = 128
SPAN = 96
GROUP = 4
BLOCK = GROUP * SPAN
CTX = ("z", "xl", "c")
TEN = ("xh", "y")
MASKED = -1e30


def brought(n_z):
    far = n_z // 2
    steps = [0] + [s * k for k in range(1, far) for s in (1, -1)]
    return [(k, side) for k in steps for side in (0, 1)] + [(far, 0), (far, 1)]


def attention_kernel(n_blocks, table_ref, limit_ref, q_ref, g_ref, *refs):
    blocks, refs = refs[:n_blocks], refs[n_blocks:]
    att_ref, gq_ref = refs[:2]
    outs, (kv_s, acc_s, s_s, qs, gs, o_s) = refs[2:8], refs[8:]
    halves = q_ref.shape[0] // SPAN
    n_spans = sum(out.shape[0] for out in outs)
    heads = q_ref.shape[1] // HEAD
    rows = heads * SPAN
    wide = qs.shape[0]
    inv_root = 1.0 / math.sqrt(HEAD)
    scale2 = inv_root * math.log2(math.e)

    def span_at(entry):
        return pl.ds(pl.multiple_of(table_ref[entry] * SPAN, SPAN), SPAN)

    entry = 0
    for ref in blocks:
        for j in range(ref.shape[0]):
            for i in range(halves):
                kv_s[span_at(entry), :] = ref[j, i * SPAN : (i + 1) * SPAN]
                entry += 1

    def clear(b, carry):
        acc_s[pl.ds(pl.multiple_of(b * BLOCK, BLOCK), BLOCK), :] = jnp.zeros(
            (BLOCK, 2 * HEAD), jnp.float32
        )
        return carry

    lax.fori_loop(0, n_spans // GROUP, clear, 0)
    qs[rows:, :] = jnp.zeros((wide - rows, HEAD), qs.dtype)
    gs[rows:, :] = jnp.zeros((wide - rows, HEAD), gs.dtype)

    def one_span(i, done):
        own = pl.ds(pl.multiple_of(i * SPAN, SPAN), SPAN)
        for h in range(heads):
            qs[h * SPAN : (h + 1) * SPAN, :] = q_ref[own, h * HEAD : (h + 1) * HEAD]
            gs[h * SPAN : (h + 1) * SPAN, :] = g_ref[own, h * HEAD : (h + 1) * HEAD]
        lo, full_lo, full_hi, hi = (table_ref[2 * n_spans + 4 * i + j] for j in range(4))
        first, last = limit_ref[i, 0], limit_ref[i, 1]

        def block(b):
            return pl.ds(pl.multiple_of(b * BLOCK, BLOCK), BLOCK)

        def score(masked, b, top):
            s = lax.dot_general(
                kv_s[block(b), :HEAD], qs[...], (((1,), (1,)), ((), ())),
                preferred_element_type=jnp.float32,
            ) * scale2
            if masked:
                pos = lax.broadcasted_iota(jnp.int32, s.shape, 0) + b * BLOCK
                s = jnp.where((pos >= first) & (pos <= last), s, MASKED)
            s_s[block(b), :] = s
            return jnp.maximum(top, jnp.max(s.reshape(BLOCK // 8, 8, wide), axis=0))

        masked, plain = (functools.partial(score, m) for m in (True, False))
        top = jnp.full((8, wide), MASKED, jnp.float32)
        top = lax.fori_loop(lo, full_lo, masked, top)
        top = lax.fori_loop(full_lo, full_hi, plain, top)
        top = lax.fori_loop(full_hi, hi, masked, top)
        top = jnp.max(top, axis=0, keepdims=True)
        o_s[...] = jnp.zeros_like(o_s)

        def weigh(b, total):
            e = jnp.exp2(s_s[block(b), :] - top)
            s_s[block(b), :] = e
            o_s[...] += lax.dot_general(
                kv_s[block(b), HEAD:], e.astype(jnp.bfloat16), (((0,), (0,)), ((), ())),
                preferred_element_type=jnp.float32,
            )
            return total + jnp.sum(e.reshape(BLOCK // 8, 8, wide), axis=0)

        total = lax.fori_loop(lo, hi, weigh, jnp.zeros((8, wide), jnp.float32))
        share = 1.0 / jnp.sum(total, axis=0, keepdims=True)
        att = (o_s[...] * share).astype(jnp.bfloat16).astype(jnp.float32)
        delta = jnp.sum(att * gs[...].astype(jnp.float32).T, axis=0, keepdims=True)
        att = att.T.astype(jnp.bfloat16)
        for h in range(heads):
            att_ref[own, h * HEAD : (h + 1) * HEAD] = att[h * SPAN : (h + 1) * SPAN]
        o_s[...] = jnp.zeros_like(o_s)

        def back(b, carry):
            k = kv_s[block(b), :HEAD]
            v = kv_s[block(b), HEAD:]
            p = s_s[block(b), :] * share
            grad_p = lax.dot_general(
                v, gs[...], (((1,), (1,)), ((), ())), preferred_element_type=jnp.float32
            )
            grad_s = (p * (grad_p - delta) * inv_root).astype(jnp.bfloat16)
            acc_s[block(b), HEAD:] += jnp.dot(
                p.astype(jnp.bfloat16), gs[...], preferred_element_type=jnp.float32
            )
            acc_s[block(b), :HEAD] += jnp.dot(
                grad_s, qs[...], preferred_element_type=jnp.float32
            )
            o_s[...] += lax.dot_general(
                k, grad_s, (((0,), (0,)), ((), ())), preferred_element_type=jnp.float32
            )
            return carry

        lax.fori_loop(lo, hi, back, 0)
        grad_q = o_s[...].T.astype(jnp.bfloat16)
        for h in range(heads):
            gq_ref[own, h * HEAD : (h + 1) * HEAD] = grad_q[h * SPAN : (h + 1) * SPAN]
        return done

    lax.fori_loop(0, halves, one_span, 0)

    entry = n_spans
    for out in outs:

        def send(j, carry, out=out, entry=entry):
            out[j] = acc_s[span_at(entry + j), :].astype(jnp.bfloat16)
            return carry

        lax.fori_loop(0, out.shape[0], send, 0)
        entry += out.shape[0]


def on_chip(arrays):
    return [pltpu.with_memory_space_constraint(x, pltpu.VMEM) for x in arrays]


def attend(table, limit, queries, grads, blocks):
    smem = pl.BlockSpec(memory_space=pltpu.SMEM)
    vmem = pl.BlockSpec(memory_space=pltpu.VMEM)
    shard = queries.shape[0]
    n_slots = sum(x.shape[0] for x in blocks) // 4
    tokens = 4 * n_slots * shard
    wide = limit.shape[-1]

    def part(n):
        return pltpu.VMEM((n * n_slots, SPAN, 2 * HEAD), jnp.bfloat16)

    rows_like = jax.ShapeDtypeStruct(queries.shape, jnp.bfloat16)
    return pl.pallas_call(
        functools.partial(attention_kernel, len(blocks)),
        name="attention",
        out_shape=(rows_like, rows_like) + (part(2), part(1), part(1)) * 2,
        in_specs=[smem] + [vmem] * (3 + len(blocks)),
        out_specs=[vmem] * 8,
        compiler_params=pltpu.CompilerParams(vmem_limit_bytes=28 * 2**20),
        scratch_shapes=[
            pltpu.VMEM((tokens, 2 * HEAD), jnp.bfloat16),
            pltpu.VMEM((tokens, 2 * HEAD), jnp.float32),
            pltpu.VMEM((tokens, wide), jnp.float32),
            pltpu.VMEM((wide, HEAD), jnp.bfloat16),
            pltpu.VMEM((wide, HEAD), jnp.bfloat16),
            pltpu.VMEM((HEAD, wide), jnp.float32),
        ],
    )(table, limit, queries, grads, *on_chip(blocks))


def strips_kernel(at_ref, rows_ref, *refs):
    outs, turned = refs[:4], refs[4]
    n_z, part, _ = outs[0].shape
    for i in range(n_z):
        turned[...] = rows_ref[:, i * 4 * part : (i + 1) * 4 * part].astype(jnp.float32).T
        for k, out in enumerate(outs):
            start = pl.multiple_of(at_ref[k] * part, 16)
            out[i] = turned[pl.ds(start, part), :].astype(jnp.bfloat16)


def strips_of(at, rows, n_z):
    shard, width = rows.shape
    part = width // (4 * n_z)
    vmem = pl.BlockSpec(memory_space=pltpu.VMEM)
    return pl.pallas_call(
        strips_kernel,
        name="strips",
        out_shape=(jax.ShapeDtypeStruct((n_z, part, shard), jnp.bfloat16),) * 4,
        in_specs=[pl.BlockSpec(memory_space=pltpu.SMEM), vmem],
        out_specs=[vmem] * 4,
        scratch_shapes=[pltpu.VMEM((4 * part, shard), jnp.float32)],
        compiler_params=pltpu.CompilerParams(vmem_limit_bytes=10 * 2**20),
    )(at, rows)


def grad_w_kernel(z_ref, *refs):
    strips, grads, outs = refs[:4], refs[4:8], refs[8:]
    n_z = strips[0].shape[0]
    for k, out in enumerate(outs):
        i = lax.rem(z_ref[0] + k, n_z)
        total = jnp.dot(strips[0][i], grads[0][...], preferred_element_type=jnp.float32)
        for x, y in zip(strips[1:], grads[1:]):
            total += jnp.dot(x[i], y[...], preferred_element_type=jnp.float32)
        out[...] = total.astype(out.dtype)


def grad_w_parts(z, strips, grads):
    n_z, part, _ = strips[0].shape
    vmem = pl.BlockSpec(memory_space=pltpu.VMEM)
    shape = (part, grads[0].shape[1])
    return pl.pallas_call(
        grad_w_kernel,
        name="grad_w",
        out_shape=(jax.ShapeDtypeStruct(shape, jnp.float32),)
        + (jax.ShapeDtypeStruct(shape, jnp.bfloat16),) * (n_z - 1),
        in_specs=[pl.BlockSpec(memory_space=pltpu.SMEM)] + [vmem] * 8,
        out_specs=[vmem] * n_z,
        compiler_params=pltpu.CompilerParams(vmem_limit_bytes=10 * 2**20),
    )(z, *strips, *grads)


def grad_rows_kernel(grad_ref, w_ref, out_ref):
    step = w_ref.shape[0] // 8
    for i in range(8):
        at = slice(i * step, (i + 1) * step)
        out_ref[:, at] = lax.dot_general(
            grad_ref[...], w_ref[at, :], (((1,), (1,)), ((), ())),
            preferred_element_type=jnp.float32,
        ).astype(out_ref.dtype)


def grad_rows_of(grad_kv, weights):
    vmem = pl.BlockSpec(memory_space=pltpu.VMEM)
    return pl.pallas_call(
        grad_rows_kernel,
        name="grad_rows",
        out_shape=pltpu.VMEM((grad_kv.shape[0], weights.shape[0]), jnp.bfloat16),
        in_specs=[vmem, vmem],
        out_specs=vmem,
        compiler_params=pltpu.CompilerParams(vmem_limit_bytes=8 * 2**20),
    )(*on_chip((grad_kv, weights)))


def total_kernel(terms_ref, out_ref):
    total = terms_ref[0].astype(jnp.float32)
    for i in range(1, terms_ref.shape[0]):
        total += terms_ref[i].astype(jnp.float32)
    out_ref[...] = total.astype(out_ref.dtype)


def total_of(terms):
    vmem = pl.BlockSpec(memory_space=pltpu.VMEM)
    return pl.pallas_call(
        total_kernel,
        name="total",
        out_shape=jax.ShapeDtypeStruct(terms.shape[1:], terms.dtype),
        in_specs=[vmem],
        out_specs=vmem,
        compiler_params=pltpu.CompilerParams(vmem_limit_bytes=4 * 2**20),
    )(*on_chip((terms,)))


def on_device(
    n_z, activations, queries, key_weight, value_weight, output_gradient, span_order, doc_ids
):
    n_ten = 8
    own_rows, width = activations.shape
    shard = own_rows * n_ten
    spans = span_order.shape[0]
    per_shard = shard // SPAN
    heads = queries.shape[1] // HEAD
    z, xl, c = (lax.axis_index(a) for a in CTX)
    swap = [(0, 1), (1, 0)]
    up = [(i, (i + 1) % n_z) for i in range(n_z)]
    down = [(i, (i - 1) % n_z) for i in range(n_z)]

    dz = jnp.array([d for d, _ in brought(n_z)], jnp.int32)
    side = jnp.array([x for _, x in brought(n_z)], jnp.int32)
    halves = jnp.arange(per_shard, dtype=jnp.int32)
    in_near = (((z - dz) % n_z) * 4 + (xl ^ side) * 2)[:, None] * per_shard + halves[None, :]
    steps = jnp.arange(n_z, dtype=jnp.int32)
    below = ((z - steps) % n_z) * 4

    def sent_at(core):
        own_side = ((below + xl * 2 + core)[:, None] * per_shard + halves[None, :]).reshape(-1)
        first = (below + (1 - xl) * 2 + core) * per_shard
        second = (steps * 4 + (1 - xl) * 2 + core) * per_shard + 1
        return [own_side, first, second]

    spans_of = jnp.concatenate(
        [
            (in_near + c * per_shard).reshape(-1),
            (in_near + (1 - c) * per_shard).reshape(-1),
            *sent_at(c),
            *sent_at(1 - c),
        ]
    )
    ids = jnp.arange(spans, dtype=jnp.int32)
    places = jnp.sum(jnp.where(spans_of[:, None] == ids[None, :], span_order[None, :], 0), axis=1)
    first_row = (z * 4 + xl * 2 + c) * shard
    my_order = lax.dynamic_slice_in_dim(span_order, first_row // SPAN, per_shard)
    my_doc = lax.dynamic_slice_in_dim(doc_ids, first_row, shard)
    my_first = jnp.sum((doc_ids[None, :] < my_doc[:, None]).astype(jnp.int32), axis=1)
    my_first = my_first.reshape(per_shard, SPAN)
    my_pos = my_order[:, None] * SPAN + jnp.arange(SPAN, dtype=jnp.int32)[None, :]
    lo, hi = jnp.min(my_first, axis=1) // BLOCK, my_pos[:, -1] // BLOCK + 1
    full_lo = jnp.minimum((jnp.max(my_first, axis=1) + BLOCK - 1) // BLOCK, hi)
    full_hi = jnp.maximum((my_pos[:, 0] + 1) // BLOCK, full_lo)
    bound = jnp.stack([lo, full_lo, full_hi, hi], axis=1)
    table = jnp.concatenate([places, bound.reshape(-1)])
    wide = -(-heads * SPAN // 128) * 128
    pad = wide - heads * SPAN
    limit = jnp.stack(
        [
            jnp.pad(jnp.tile(my_first, (1, heads)), ((0, 0), (0, pad)), constant_values=1),
            jnp.pad(jnp.tile(my_pos, (1, heads)), ((0, 0), (0, pad))),
        ],
        axis=1,
    ).reshape(per_shard, 2, 1, wide)

    def low(x):
        return x.astype(jnp.bfloat16)

    def add(x, y):
        return low(x.astype(jnp.float32) + y.astype(jnp.float32))

    rows = lax.all_to_all(
        jnp.broadcast_to(activations[None], (n_ten, own_rows, width)), TEN, 0, 0
    ).reshape(shard, width)
    weights = jnp.concatenate([key_weight, value_weight], axis=1)
    rows, weights, table, limit = lax.optimization_barrier((rows, weights, table, limit))
    kv = low(jnp.dot(rows, weights, preferred_element_type=jnp.float32))
    beside = lax.ppermute(kv, "xl", swap)
    pair = jnp.stack([kv, beside])
    near = [pair]
    a = b = pair
    for _ in range(1, n_z // 2):
        a = lax.ppermute(a, "z", up)
        b = lax.ppermute(b, "z", down)
        near += [a, b]
    a = lax.ppermute(a[:1], "z", up)
    b = lax.ppermute(b[1:], "z", down)
    near = [jnp.concatenate(near[:5]), jnp.concatenate(near[5:]), jnp.concatenate([a, b])]
    far = []
    for x in near:
        far.append(lax.ppermute(x, "c", swap))

    around = jnp.stack([xl * 2 + c, xl * 2 + 1 - c, (1 - xl) * 2 + c, (1 - xl) * 2 + 1 - c])
    keep, give_c, give_x, give_cx = strips_of(around, rows, n_z)
    got_x = lax.ppermute(give_x, "xl", swap)
    got_c, got_cx = (lax.ppermute(t, "c", swap) for t in (give_c, give_cx))
    got_cx = lax.ppermute(got_cx, "xl", swap)
    strips = (keep, got_c, got_x, got_cx)

    attended, grad_queries, *parts = attend(table, limit, queries, output_gradient, [*near, *far])

    near_own, near_0, near_1, far_own, far_0, far_1 = parts
    far_0 = lax.ppermute(far_0, "c", swap)
    far_1 = lax.ppermute(far_1, "c", swap)
    far_own = lax.ppermute(far_own, "c", swap)
    part_0 = lax.ppermute(add(near_0, far_0), "xl", swap)
    part_1 = lax.all_to_all(add(near_1, far_1), "z", 0, 0)
    part = near_own.astype(jnp.float32) + far_own.astype(jnp.float32)
    part = part.reshape(n_z, per_shard, SPAN, 2 * HEAD)
    part += jnp.pad(part_0[:, None].astype(jnp.float32), ((0, 0), (0, 1), (0, 0), (0, 0)))
    own = part[0]
    for k in sorted(range(1, n_z), key=lambda k: -min(k, n_z - k)):
        shift = [(i, (i - k) % n_z) for i in range(n_z)]
        own = own + lax.ppermute(low(part[k]), "z", shift).astype(jnp.float32)
    part_1 = low(jnp.sum(part_1.astype(jnp.float32), axis=0))
    part_1 = lax.ppermute(part_1, "xl", swap)
    own = own + jnp.pad(part_1[None].astype(jnp.float32), ((1, 0), (0, 0), (0, 0)))
    grad_kv = low(own).reshape(shard, 2 * HEAD)

    beside = lax.ppermute(grad_kv, "xl", swap)
    across = lax.ppermute(grad_kv, "c", swap)
    corner = lax.ppermute(beside, "c", swap)
    grad_rows = grad_rows_of(grad_kv, weights)
    terms = lax.all_to_all(grad_rows.reshape(n_ten, own_rows, width), TEN, 0, 0)

    grad_w, *sent = grad_w_parts(z[None], strips, (grad_kv, across, beside, corner))
    sent = sorted(enumerate(sent, 1), key=lambda kx: -min(kx[0], n_z - kx[0]))
    for k, x in sent:
        shift = [(i, (i + k) % n_z) for i in range(n_z)]
        grad_w = grad_w + lax.ppermute(x, "z", shift).astype(jnp.float32)
    grad_inputs = total_of(terms)
    return attended, grad_queries, grad_inputs, grad_w[:, :HEAD], grad_w[:, HEAD:]


def solution(mesh):
    n_z = mesh.shape["context"] // 4
    fine = Mesh(mesh.devices.reshape(n_z, 2, 2, 2, 4), CTX + TEN)

    def body(*args):
        return on_device(n_z, *args)

    return jax.shard_map(
        body,
        mesh=fine,
        in_specs=(
            P(CTX + TEN, None),
            P(CTX, TEN),
            P(None, TEN),
            P(None, TEN),
            P(CTX, TEN),
            P(),
            P(),
        ),
        out_specs=(
            P(CTX, TEN),
            P(CTX, TEN),
            P(CTX + TEN, None),
            P(CTX, TEN),
            P(CTX, TEN),
        ),
        check_vma=False,
    )
```
